32 devices in a mesh: dp: 8 (over z, y), group: 4 (over x, core).
Axes of the slice: x: 2, y: 2, z: 4, core: 2. Of those that a mesh axis runs over, the one named last changes fastest.
Arguments:
- tokens: bfloat16 [4096, 1088], P(('dp', 'group')), may hold values from -6 to 6
- cotangent: bfloat16 [4096, 1088], P(('dp', 'group')), may hold values from -6 to 6
- segment_ids: int32 [4096], P(('dp', 'group')), may hold values from 0 to 7, never falling along the last dimension, each value on 1 to 1024 neighbouring positions
- w_qkv: float32 [1088, 3264], P('group', 'dp'), may hold values from -0.1875 to 0.1875
- w_out: float32 [1088, 1088], P('group', 'dp'), may hold values from -0.1875 to 0.1875
- w_up: float32 [1088, 4352], P('group', 'dp'), may hold values from -0.1875 to 0.1875
- w_down: float32 [4352, 1088], P('group', 'dp'), may hold values from -0.09375 to 0.09375
- vectors: float32 [12, 1088], P(None, 'group'), may hold values from -1.5 to 1.5, as said below
- m_qkv: float32 [1088, 3264], P('group', 'dp'), may hold values from -24 to 24
- m_out: float32 [1088, 1088], P('group', 'dp'), may hold values from -6 to 6
- m_up: float32 [1088, 4352], P('group', 'dp'), may hold values from -20 to 20
- m_down: float32 [4352, 1088], P('group', 'dp'), may hold values from -40 to 40
- m_vec: float32 [12, 1088], P(None, 'group'), may hold values from -96 to 96
- v_qkv: float32 [1088, 3264], P('group', 'dp'), may hold values from 0.8192 to 8.192
- v_out: float32 [1088, 1088], P('group', 'dp'), may hold values from 0.4096 to 4.096
- v_up: float32 [1088, 4352], P('group', 'dp'), may hold values from 0.4096 to 1.6384
- v_down: float32 [4352, 1088], P('group', 'dp'), may hold values from 1.2288 to 4.9152
- v_vec: float32 [12, 1088], P(None, 'group'), may hold values from 8.192 to 81.92
Outputs:
- output: bfloat16 [4096, 1088], P(('dp', 'group'))
- input_grad: float32 [4096, 1088], P(('dp', 'group'))
- grad_qkv: float32 [1088, 3264], P('group', 'dp')
- grad_out: float32 [1088, 1088], P('group', 'dp')
- grad_up: float32 [1088, 4352], P('group', 'dp')
- grad_down: float32 [4352, 1088], P('group', 'dp')
- grad_vec: float32 [12, 1088], P(None, 'group')
- new_qkv: float32 [1088, 3264], P('group', 'dp')
- new_out: float32 [1088, 1088], P('group', 'dp')
- new_up: float32 [1088, 4352], P('group', 'dp')
- new_down: float32 [4352, 1088], P('group', 'dp')
- new_vec: float32 [12, 1088], P(None, 'group')
- new_m_qkv: float32 [1088, 3264], P('group', 'dp')
- new_m_out: float32 [1088, 1088], P('group', 'dp')
- new_m_up: float32 [1088, 4352], P('group', 'dp')
- new_m_down: float32 [4352, 1088], P('group', 'dp')
- new_m_vec: float32 [12, 1088], P(None, 'group')
- new_v_qkv: float32 [1088, 3264], P('group', 'dp')
- new_v_out: float32 [1088, 1088], P('group', 'dp')
- new_v_up: float32 [1088, 4352], P('group', 'dp')
- new_v_down: float32 [4352, 1088], P('group', 'dp')
- new_v_vec: float32 [12, 1088], P(None, 'group')
The draws below stay inside these ranges and needn't reach their ends.
Inputs may be any that keep to these rules, and one draw needn't show every extreme that they name: `segment_ids`: ids never fall along the stream; each id covers 1 to 1024 consecutive tokens, and one covers exactly 1024. `vectors`: rows 0 and 5 lie between 0.5 and 1.5.
All inputs are finite; a program needn't handle non-finite values.
Results may differ from the reference program's by a relative error of at most 0.023.
Values may be sent and summed in bfloat16 or wider, within the bound.
No kernel may reach another device: no remote copies, remote signals or barrier semaphores. Data moves between devices by JAX's collectives and lax.ppermute only.
A program may use at most 256 MiB of HBM per device.

```python
import math
import jax
import jax.numpy as jnp
import numpy as np
from jax import lax

D = 1088
HEADS = 17
HEAD_DIM = 64
FF = 4352
TOK_DEV = 128
SEG_MAX = 1024
ADAM_STEP = 3
REACH = 8
TOKENS = 4096
SEGMENTS = 8


def draw_vectors(key, part):
    gain_key, other_key = jax.random.split(jax.random.fold_in(key, 11))
    gain_rows = jax.random.uniform(gain_key, (2, D), jnp.float32, 0.6, 1.4)
    other_rows = jnp.clip(0.5 * jax.random.normal(other_key, (10, D), jnp.float32), -1.5, 1.5)
    return jnp.concatenate([gain_rows[0:1], other_rows[0:4], gain_rows[1:2], other_rows[4:10]], axis=0)


def level_of(stream_key, dims, cuts, smallest, high):
    def one(position, parts):
        steps = jax.random.uniform(jax.random.fold_in(jax.random.fold_in(stream_key, 6), position), (parts,), jnp.float32, smallest / len(cuts), high / len(cuts))
        return jnp.repeat(jnp.exp(steps), dims[position] // parts).reshape((-1,) + (1,) * (len(dims) - position - 1))

    level = one(*cuts[0])
    for cut in cuts[1:]:
        level = level * one(*cut)
    return level


def profile(amount, total, bound, slope):
    weights = [(1 << 20) // math.isqrt(grade ** slope) + 1 for grade in range(2, amount + 1)]
    spare, given = total - bound - (amount - 1), [1] * (amount - 1)
    while spare > 0:
        candidates = [i for i in range(amount - 1) if given[i] < bound]
        whole, left = sum([weights[i] for i in candidates]), spare
        for i in candidates:
            more = min(bound - given[i], max(1, left * weights[i] // whole), spare)
            given[i] = given[i] + more
            spare = spare - more
    return np.array([bound] + given)


def uneven(key, amount, total, most, slope):
    if amount == 2:
        one = jax.random.randint(key, (), max(1, total - most), min(most, total - 1) + 1)
        return jnp.stack([one, total - one])
    lengths = jnp.asarray(profile(amount, total, most, slope), jnp.int32)
    twos = (amount - 1) // 2
    giver, sink = lengths[1:1 + 2 * twos:2], lengths[2:2 + 2 * twos:2]
    room = jnp.minimum(giver - 1, most - sink)
    shifted = jax.random.randint(jax.random.fold_in(key, 1), (twos,), 0, 1 << 20) % (room + 1)
    lengths = lengths.at[1:1 + 2 * twos:2].set(giver - shifted).at[2:2 + 2 * twos:2].set(sink + shifted)
    return lengths[jax.random.permutation(jax.random.fold_in(key, 2), amount)]


def gaussian(own_key, shape, width, most, shards=(), kind=jnp.bfloat16):
    level = level_of(own_key, shape, shards, -0.22, 0.18) if shards else 1.0
    result = jax.random.normal(own_key, shape, jnp.float32) * width * level
    return jnp.minimum(jnp.maximum(result, -most), most).astype(kind)


def setup_inputs(seed: int = 0) -> dict:
    arg_keys = jax.random.split(jax.random.key(seed), 19)
    tokens = gaussian(arg_keys[0], (TOKENS, D), 1.0, 6.0, ((0, 32),))
    cotangent = gaussian(arg_keys[1], (TOKENS, D), 1.0, 6.0, ((0, 32),))
    segment_ids = jnp.searchsorted(jnp.cumsum(uneven(arg_keys[2], SEGMENTS, TOKENS, SEG_MAX, 2)), jnp.arange(TOKENS), side="right").astype(jnp.int32)
    w_qkv = gaussian(arg_keys[3], (D, 3 * D), D ** -0.5, 0.1875, ((0, 4), (1, 8)), jnp.float32)
    w_out = gaussian(arg_keys[4], (D, D), D ** -0.5, 0.1875, ((0, 4), (1, 8)), jnp.float32)
    w_up = gaussian(arg_keys[5], (D, FF), D ** -0.5, 0.1875, ((0, 4), (1, 8)), jnp.float32)
    w_down = gaussian(arg_keys[6], (FF, D), FF ** -0.5, 0.09375, ((0, 4), (1, 8)), jnp.float32)
    vectors = draw_vectors(jax.random.fold_in(arg_keys[18], 71), 0)
    m_qkv = gaussian(arg_keys[8], (D, 3 * D), (0.06 * TOKENS ** 0.5), 24.0, ((0, 4), (1, 8)), jnp.float32)
    m_out = gaussian(arg_keys[9], (D, D), (0.03 * TOKENS ** 0.5), 6.0, ((0, 4), (1, 8)), jnp.float32)
    m_up = gaussian(arg_keys[10], (D, FF), (0.05 * TOKENS ** 0.5), 20.0, ((0, 4), (1, 8)), jnp.float32)
    m_down = gaussian(arg_keys[11], (FF, D), (0.1 * TOKENS ** 0.5), 40.0, ((0, 4), (1, 8)), jnp.float32)
    m_vec = gaussian(arg_keys[12], (12, D), (0.25 * TOKENS ** 0.5), 96.0, ((1, 4),), jnp.float32)
    v_qkv = jnp.clip(jnp.exp(math.log(8.192) - 2.3025852 * jax.random.uniform(arg_keys[13], (D, 3 * D), jnp.float32) ** level_of(arg_keys[13], (D, 3 * D), ((0, 4), (1, 8)), -0.2, 0.2)), 0.8192, 8.192)
    v_out = jnp.clip(jnp.exp(math.log(4.096) - 2.3025852 * jax.random.uniform(arg_keys[14], (D, D), jnp.float32) ** level_of(arg_keys[14], (D, D), ((0, 4), (1, 8)), -0.2, 0.2)), 0.4096, 4.096)
    v_up = jnp.clip(jnp.exp(math.log(1.6384) - 1.3862944 * jax.random.uniform(arg_keys[15], (D, FF), jnp.float32) ** level_of(arg_keys[15], (D, FF), ((0, 4), (1, 8)), -0.2, 0.2)), 0.4096, 1.6384)
    v_down = jnp.clip(jnp.exp(math.log(4.9152) - 1.3862944 * jax.random.uniform(arg_keys[16], (FF, D), jnp.float32) ** level_of(arg_keys[16], (FF, D), ((0, 4), (1, 8)), -0.2, 0.2)), 1.2288, 4.9152)
    v_vec = jnp.clip(jnp.exp(math.log(81.92) - 2.30258502 * jax.random.uniform(arg_keys[17], (12, D), jnp.float32) ** level_of(arg_keys[17], (12, D), ((1, 4),), -0.2, 0.2)), 8.192, 81.92)
    return {"tokens": tokens, "cotangent": cotangent, "segment_ids": segment_ids, "w_qkv": w_qkv, "w_out": w_out, "w_up": w_up, "w_down": w_down, "vectors": vectors, "m_qkv": m_qkv, "m_out": m_out, "m_up": m_up, "m_down": m_down, "m_vec": m_vec, "v_qkv": v_qkv, "v_out": v_out, "v_up": v_up, "v_down": v_down, "v_vec": v_vec}


def rounded(values):
    return lax.optimization_barrier(values.astype(jnp.bfloat16)).astype(jnp.float32)

def layer_norm(rows):
    mean_rows = lax.optimization_barrier(jnp.mean(rows, axis=-1, keepdims=True))
    centered = rows - mean_rows
    variance = lax.optimization_barrier(jnp.mean(centered * centered, axis=-1, keepdims=True))
    inv_std = lax.rsqrt(variance + 1e-05)
    return (centered * inv_std, inv_std)

def norm_back(d_normed, normed, inv_std):
    return inv_std * (d_normed - lax.optimization_barrier(jnp.mean(d_normed, axis=-1, keepdims=True)) - normed * lax.optimization_barrier(jnp.mean(d_normed * normed, axis=-1, keepdims=True)))

def gelu_parts(pre_act):
    gelu_scale = 0.7978845608028654
    cubic_term = 0.044715 * pre_act * pre_act
    argument = gelu_scale * pre_act * (1.0 + cubic_term)
    tangent = jnp.tanh(argument)
    activated = 0.5 * pre_act * (1.0 + tangent)
    derivative = 0.5 * (1.0 + tangent) + 0.5 * pre_act * (1.0 - tangent * tangent) * gelu_scale * (1.0 + 3.0 * cubic_term)
    return (activated, derivative)

def adamw_update(weight_now, first_mom, second_mom, gradient, decay_rate):
    new_first = 0.9 * first_mom + 0.1 * gradient
    new_second = 0.999 * second_mom + 0.001 * gradient * gradient
    step_size = new_first / (1.0 - 0.9 ** ADAM_STEP) / (jnp.sqrt(new_second / (1.0 - 0.999 ** ADAM_STEP)) + 1e-08)
    return (weight_now - 0.03 * (step_size + decay_rate * weight_now), new_first, new_second)

def reference(tokens, cotangent, segment_ids, w_qkv, w_out, w_up, w_down, vectors, m_qkv, m_out, m_up, m_down, m_vec, v_qkv, v_out, v_up, v_down, v_vec):
    qkv_used = w_qkv.astype(jnp.bfloat16)
    out_used = w_out.astype(jnp.bfloat16)
    up_used = w_up.astype(jnp.bfloat16)
    down_used = w_down.astype(jnp.bfloat16)
    vec_used = rounded(vectors)
    norm_gain = vec_used[0]
    norm_shift = vec_used[1]
    bias_query = vec_used[2]
    bias_value = vec_used[3]
    bias_out = vec_used[4]
    gain_two = vec_used[5]
    shift_two = vec_used[6]
    bias_down = vec_used[7]
    bias_up = vec_used[8:12].reshape(FF)
    score_scale = HEAD_DIM ** (-0.5)
    tokens_wide = tokens.astype(jnp.float32)
    normed, inv_std = layer_norm(tokens_wide)
    hidden = (normed * norm_gain + norm_shift).astype(jnp.bfloat16)
    qkv = jnp.dot(hidden, qkv_used, preferred_element_type=jnp.float32)
    query_rows = ((qkv[:, :D] + bias_query) * score_scale).astype(jnp.bfloat16)
    key_rows = qkv[:, D:2 * D].astype(jnp.bfloat16)
    value_rows = (qkv[:, 2 * D:] + bias_value).astype(jnp.bfloat16)
    pad_rows = REACH * TOK_DEV
    window = (REACH + 1) * TOK_DEV
    block_count = TOKENS // TOK_DEV
    key_pad = jnp.concatenate([jnp.zeros((pad_rows, D), jnp.bfloat16), key_rows], 0)
    value_pad = jnp.concatenate([jnp.zeros((pad_rows, D), jnp.bfloat16), value_rows], 0)
    seg_pad = jnp.concatenate([jnp.full((pad_rows,), -1, jnp.int32), segment_ids.astype(jnp.int32)], 0)

    def window_parts(block_id):
        first_row = (block_id * TOK_DEV).astype(jnp.int32)
        query_blk = lax.dynamic_slice_in_dim(query_rows, first_row, TOK_DEV, 0).astype(jnp.float32).reshape(TOK_DEV, HEADS, HEAD_DIM)
        key_blk = lax.dynamic_slice_in_dim(key_pad, first_row, window, 0).astype(jnp.float32).reshape(window, HEADS, HEAD_DIM)
        value_blk = lax.dynamic_slice_in_dim(value_pad, first_row, window, 0).astype(jnp.float32).reshape(window, HEADS, HEAD_DIM)
        seg_query = lax.dynamic_slice_in_dim(segment_ids.astype(jnp.int32), first_row, TOK_DEV, 0)
        seg_keys = lax.dynamic_slice_in_dim(seg_pad, first_row, window, 0)
        query_pos = jnp.arange(TOK_DEV, dtype=jnp.int32) + pad_rows
        key_pos = jnp.arange(window, dtype=jnp.int32)
        allowed = (seg_query[:, None] == seg_keys[None, :]) & (key_pos[None, :] <= query_pos[:, None])
        scores = jnp.einsum('qhd,khd->hqk', query_blk, key_blk)
        weights = jnp.where(allowed[None], jnp.exp(scores), jnp.float32(0.0))
        return (query_blk, key_blk, value_blk, weights)

    def forward_block(block_id):
        query_blk, key_blk, value_blk, weights = window_parts(block_id)
        denominator = lax.optimization_barrier(jnp.sum(weights, axis=2))
        numerator = jnp.einsum('hqk,khd->qhd', rounded(weights), value_blk)
        return (numerator / denominator.T[:, :, None], denominator)
    context_blocks, denominators = lax.map(forward_block, jnp.arange(block_count, dtype=jnp.int32))
    context = context_blocks.reshape(TOKENS, D)
    context_b = context.astype(jnp.bfloat16)
    attended = jnp.dot(context_b, out_used, preferred_element_type=jnp.float32)
    mid = tokens_wide + (attended + bias_out)
    mlp_rows = math.gcd(TOKENS, 4096)
    mlp_blocks = TOKENS // mlp_rows

    def mlp_block(carry, items):
        grad_up_acc, grad_down_acc, bias_up_acc, gain_acc, shift_acc = carry
        mid_blk, cot_blk = items
        normed_two, inv_two = layer_norm(mid_blk)
        hidden_two = (normed_two * gain_two + shift_two).astype(jnp.bfloat16)
        pre_act = jnp.dot(hidden_two, up_used, preferred_element_type=jnp.float32) + bias_up
        activated, derivative = gelu_parts(pre_act)
        act_b = activated.astype(jnp.bfloat16)
        down_sum = jnp.dot(act_b, down_used, preferred_element_type=jnp.float32)
        out_blk = (mid_blk + (down_sum + bias_down)).astype(jnp.bfloat16)
        d_act = jnp.dot(cot_blk, down_used.T, preferred_element_type=jnp.float32)
        d_pre = d_act * derivative
        d_pre_b = d_pre.astype(jnp.bfloat16)
        d_hidden_two = jnp.dot(d_pre_b, up_used.T, preferred_element_type=jnp.float32)
        d_mid_blk = cot_blk.astype(jnp.float32) + norm_back(d_hidden_two * gain_two, normed_two, inv_two)
        grad_up_acc = grad_up_acc + jnp.dot(hidden_two.T, d_pre_b, preferred_element_type=jnp.float32)
        grad_down_acc = grad_down_acc + jnp.dot(act_b.T, cot_blk, preferred_element_type=jnp.float32)
        bias_up_acc = bias_up_acc + lax.optimization_barrier(jnp.sum(d_pre, axis=0))
        gain_acc = gain_acc + lax.optimization_barrier(jnp.sum(d_hidden_two * normed_two, axis=0))
        shift_acc = shift_acc + lax.optimization_barrier(jnp.sum(d_hidden_two, axis=0))
        return ((grad_up_acc, grad_down_acc, bias_up_acc, gain_acc, shift_acc), (out_blk, d_mid_blk))
    mlp_start = (jnp.zeros((D, FF), jnp.float32), jnp.zeros((FF, D), jnp.float32), jnp.zeros((FF,), jnp.float32), jnp.zeros((D,), jnp.float32), jnp.zeros((D,), jnp.float32))
    mlp_items = (mid.reshape(mlp_blocks, mlp_rows, D), cotangent.reshape(mlp_blocks, mlp_rows, D))
    (grad_up, grad_down, grad_bias_up, grad_gain_two, grad_shift_two), (out_blocks, d_mid_blocks) = lax.scan(mlp_block, mlp_start, mlp_items)
    output = out_blocks.reshape(TOKENS, D)
    d_mid = d_mid_blocks.reshape(TOKENS, D)
    d_mid_b = d_mid.astype(jnp.bfloat16)
    grad_bias_down = lax.optimization_barrier(jnp.sum(cotangent.astype(jnp.float32), axis=0))
    grad_bias_out = lax.optimization_barrier(jnp.sum(d_mid, axis=0))
    grad_out = jnp.dot(context_b.T, d_mid_b, preferred_element_type=jnp.float32)
    d_context = jnp.dot(d_mid_b, out_used.T, preferred_element_type=jnp.float32)
    d_context_b = d_context.astype(jnp.bfloat16)
    row_delta = lax.optimization_barrier(jnp.sum((d_context * context).reshape(TOKENS, HEADS, HEAD_DIM), axis=2))

    def backward_block(carry, block_id):
        key_acc, value_acc = carry
        query_blk, key_blk, value_blk, weights = window_parts(block_id)
        first_row = (block_id * TOK_DEV).astype(jnp.int32)
        denominator = denominators[block_id]
        probability = weights / denominator[:, :, None]
        d_ctx_blk = lax.dynamic_slice_in_dim(d_context_b, first_row, TOK_DEV, 0).astype(jnp.float32).reshape(TOK_DEV, HEADS, HEAD_DIM)
        delta_blk = lax.dynamic_slice_in_dim(row_delta, first_row, TOK_DEV, 0).T
        d_value_win = jnp.einsum('hqk,qhd->khd', rounded(probability), d_ctx_blk)
        d_prob = jnp.einsum('qhd,khd->hqk', d_ctx_blk, value_blk)
        d_score = rounded(probability * (d_prob - delta_blk[:, :, None]))
        d_query_blk = jnp.einsum('hqk,khd->qhd', d_score, key_blk) * score_scale
        d_key_win = jnp.einsum('hqk,qhd->khd', d_score, query_blk)
        key_acc = lax.dynamic_update_slice_in_dim(key_acc, lax.dynamic_slice_in_dim(key_acc, first_row, window, 0) + d_key_win.reshape(window, D), first_row, 0)
        value_acc = lax.dynamic_update_slice_in_dim(value_acc, lax.dynamic_slice_in_dim(value_acc, first_row, window, 0) + d_value_win.reshape(window, D), first_row, 0)
        return ((key_acc, value_acc), d_query_blk.reshape(TOK_DEV, D))
    start_acc = (jnp.zeros((TOKENS + pad_rows, D), jnp.float32), jnp.zeros((TOKENS + pad_rows, D), jnp.float32))
    (key_acc, value_acc), d_query_blocks = lax.scan(backward_block, start_acc, jnp.arange(block_count, dtype=jnp.int32))
    d_query = d_query_blocks.reshape(TOKENS, D)
    d_key = key_acc[pad_rows:]
    d_value = value_acc[pad_rows:]
    grad_bias_query = lax.optimization_barrier(jnp.sum(d_query, axis=0))
    grad_bias_value = lax.optimization_barrier(jnp.sum(d_value, axis=0))
    d_qkv = jnp.concatenate([d_query, d_key, d_value], axis=1).astype(jnp.bfloat16)
    grad_qkv = jnp.dot(hidden.T, d_qkv, preferred_element_type=jnp.float32)
    d_hidden = jnp.dot(d_qkv, qkv_used.T, preferred_element_type=jnp.float32)
    grad_gain = lax.optimization_barrier(jnp.sum(d_hidden * normed, axis=0))
    grad_shift = lax.optimization_barrier(jnp.sum(d_hidden, axis=0))
    input_grad = d_mid + norm_back(d_hidden * norm_gain, normed, inv_std)
    grad_vec = jnp.concatenate([jnp.stack([grad_gain, grad_shift, grad_bias_query, grad_bias_value, grad_bias_out, grad_gain_two, grad_shift_two, grad_bias_down], axis=0), grad_bias_up.reshape(4, D)], axis=0)
    new_qkv, new_m_qkv, new_v_qkv = adamw_update(w_qkv, m_qkv, v_qkv, grad_qkv, 0.1)
    new_out, new_m_out, new_v_out = adamw_update(w_out, m_out, v_out, grad_out, 0.1)
    new_up, new_m_up, new_v_up = adamw_update(w_up, m_up, v_up, grad_up, 0.1)
    new_down, new_m_down, new_v_down = adamw_update(w_down, m_down, v_down, grad_down, 0.1)
    new_vec, new_m_vec, new_v_vec = adamw_update(vectors, m_vec, v_vec, grad_vec, 0.0)
    return (output, input_grad, grad_qkv, grad_out, grad_up, grad_down, grad_vec, new_qkv, new_out, new_up, new_down, new_vec, new_m_qkv, new_m_out, new_m_up, new_m_down, new_m_vec, new_v_qkv, new_v_out, new_v_up, new_v_down, new_v_vec)
```

```python
import functools

import jax
import jax.numpy as jnp
import numpy as np
from jax import lax
from jax.experimental import pallas as pl
from jax.experimental.pallas import tpu as pltpu
from jax.sharding import PartitionSpec as P

D = 1088
HEADS = 17
HEAD_DIM = 64
FF = 4352
ADAM_STEP = 3
REACH = 8
BF = jnp.bfloat16
F32 = jnp.float32


def layer_norm(rows):
    mean_rows = jnp.mean(rows, axis=-1, keepdims=True)
    centered = rows - mean_rows
    variance = jnp.mean(centered * centered, axis=-1, keepdims=True)
    inv_std = lax.rsqrt(variance + 1e-05)
    return (centered * inv_std, inv_std)


def norm_back(d_normed, normed, inv_std):
    return inv_std * (
        d_normed
        - jnp.mean(d_normed, axis=-1, keepdims=True)
        - normed * jnp.mean(d_normed * normed, axis=-1, keepdims=True)
    )


def gelu_parts(pre_act):
    gelu_scale = 0.7978845608028654
    cubic_term = 0.044715 * pre_act * pre_act
    argument = gelu_scale * pre_act * (1.0 + cubic_term)
    tangent = jnp.tanh(argument)
    activated = 0.5 * pre_act * (1.0 + tangent)
    derivative = 0.5 * (1.0 + tangent) + 0.5 * pre_act * (1.0 - tangent * tangent) * gelu_scale * (
        1.0 + 3.0 * cubic_term
    )
    return (activated, derivative)


def adamw_update(weight_now, first_mom, second_mom, gradient, decay_rate):
    new_first = 0.9 * first_mom + 0.1 * gradient
    new_second = 0.999 * second_mom + 0.001 * gradient * gradient
    step_size = (
        new_first
        / (1.0 - 0.9**ADAM_STEP)
        / (jnp.sqrt(new_second / (1.0 - 0.999**ADAM_STEP)) + 1e-08)
    )
    return (weight_now - 0.03 * (step_size + decay_rate * weight_now), new_first, new_second)


def dot(a, b, ca, cb, out=F32):
    return lax.dot_general(a, b, (((ca,), (cb,)), ((), ())), preferred_element_type=out)


def scores_of(q, k, same, first):
    s = lax.dot_general(q, k, (((1,), (1,)), ((), ())), preferred_element_type=F32)
    rows = lax.broadcasted_iota(jnp.int32, s.shape, 0)
    cols = lax.broadcasted_iota(jnp.int32, s.shape, 1)
    return jnp.where(same & (cols <= rows + first), jnp.exp(s), F32(0.0))


def in_order_rows(g, G, T, refs, scratch):
    for n, ref in enumerate(refs):
        for j in range(G):
            at = pl.multiple_of(lax.rem(g - j + G, G) * T, T)
            scratch[(n * G + j) * T : (n * G + j + 1) * T, :] = ref[pl.ds(at, T), :]


def attn_fwd_kernel(heads, G, g_ref, q_ref, sq_ref, sk_ref, *refs):
    kv_refs, ctx_ref, kvs = refs[:-2], refs[-2], refs[-1]
    rows = q_ref.shape[0]
    width = heads * HEAD_DIM
    window = sk_ref.shape[2]

    @pl.when(pl.program_id(0) == 0)
    def _():
        in_order_rows(g_ref[0], G, rows, kv_refs, kvs)

    at = pl.ds(pl.multiple_of(pl.program_id(0) * rows, rows), window)
    same = sq_ref[...] == sk_ref[0]
    for h in range(heads):
        lanes = slice(h * HEAD_DIM, (h + 1) * HEAD_DIM)
        lanes_v = slice(width + h * HEAD_DIM, width + (h + 1) * HEAD_DIM)
        w = scores_of(q_ref[:, lanes], kvs[at, lanes], same, window - rows)
        den = jnp.sum(w, axis=1, keepdims=True)
        num = jnp.dot(w.astype(BF), kvs[at, lanes_v], preferred_element_type=F32)
        ctx_ref[:, lanes] = num / den


def attn_bwd_kernel(heads, G, parts, g_ref, q_ref, sq_ref, sk_ref, ctx_ref, dc_ref, *refs):
    kv_refs = refs[:parts]
    dq_ref = refs[parts]
    dkv_refs = refs[parts + 1 : 2 * parts + 1]
    kvs, dkvs = refs[2 * parts + 1 :]
    rows = q_ref.shape[0]
    width = heads * HEAD_DIM
    window = sk_ref.shape[2]
    g = g_ref[0]

    @pl.when(pl.program_id(0) == 0)
    def _():
        in_order_rows(g, G, rows, kv_refs, kvs)
        dkvs[...] = jnp.zeros_like(dkvs)

    at = pl.ds(pl.multiple_of(pl.program_id(0) * rows, rows), window)
    same = sq_ref[...] == sk_ref[0]
    for h in range(heads):
        lanes = slice(h * HEAD_DIM, (h + 1) * HEAD_DIM)
        lanes_v = slice(width + h * HEAD_DIM, width + (h + 1) * HEAD_DIM)
        q = q_ref[:, lanes]
        k = kvs[at, lanes]
        dc = dc_ref[:, lanes]
        w = scores_of(q, k, same, window - rows)
        p = w * (1.0 / jnp.sum(w, axis=1, keepdims=True))
        delta = jnp.sum(dc * ctx_ref[:, lanes], axis=1, keepdims=True)
        dc_b = dc.astype(BF)
        dp = dot(dc_b, kvs[at, lanes_v], 1, 1)
        ds = (p * (dp - delta)).astype(BF)
        dq_ref[:, lanes] = jnp.dot(ds, k, preferred_element_type=F32) * (HEAD_DIM**-0.5)
        dkvs[at, lanes] += dot(ds, q, 0, 0)
        dkvs[at, lanes_v] += dot(p.astype(BF), dc_b, 0, 0)

    @pl.when(pl.program_id(0) == G - 1)
    def _():
        for n, ref in enumerate(dkv_refs):
            for j in range(G):
                to = pl.multiple_of(lax.rem(g - j + G, G) * rows, rows)
                part = dkvs[(n * G + j) * rows : (n * G + j + 1) * rows, :]
                ref[pl.ds(to, rows), :] = part.astype(ref.dtype)


def attn_specs(G, T, width, window):
    turned = lambda i, g: (lax.rem(g[0] - i + G, G), 0)
    row = pl.BlockSpec((T, width), turned)
    full = pl.BlockSpec((G * T, 2 * width), lambda i, g: (0, 0))
    sq = pl.BlockSpec((T, 1), turned)
    sk = pl.BlockSpec((1, 1, window), lambda i, g: (i, 0, 0))
    return row, full, sq, sk


def attention(g, q, kvs, sq, sk, T, heads):
    total, width = q.shape
    G, window = total // T, sk.shape[2]
    row, full, sqs, sks = attn_specs(G, T, width, window)
    work = total * window * heads
    return pl.pallas_call(
        functools.partial(attn_fwd_kernel, heads, G),
        grid_spec=pltpu.PrefetchScalarGridSpec(
            num_scalar_prefetch=1,
            grid=(G,),
            in_specs=[row, sqs, sks] + [full] * len(kvs),
            out_specs=row,
            scratch_shapes=[pltpu.VMEM((len(kvs) * total, 2 * width), BF)],
        ),
        out_shape=jax.ShapeDtypeStruct((total, width), F32),
        cost_estimate=pl.CostEstimate(
            flops=4 * work * HEAD_DIM, bytes_accessed=18 * total * width, transcendentals=work
        ),
        name="attention",
    )(g, q, sq, sk, *kvs)


def attention_back(g, q, kvs, sq, sk, ctx, d_ctx, T, heads):
    total, width = q.shape
    G, window = total // T, sk.shape[2]
    parts = len(kvs)
    row, full, sqs, sks = attn_specs(G, T, width, window)
    work = total * window * heads
    return pl.pallas_call(
        functools.partial(attn_bwd_kernel, heads, G, parts),
        grid_spec=pltpu.PrefetchScalarGridSpec(
            num_scalar_prefetch=1,
            grid=(G,),
            in_specs=[row, sqs, sks, row, row] + [full] * parts,
            out_specs=[row] + [full] * parts,
            scratch_shapes=[
                pltpu.VMEM((parts * total, 2 * width), BF),
                pltpu.VMEM((parts * total, 2 * width), F32),
            ],
        ),
        out_shape=[jax.ShapeDtypeStruct((total, width), F32)]
        + [
            jax.ShapeDtypeStruct((total, 2 * width), F32 if n == parts - 1 else BF)
            for n in range(parts)
        ],
        cost_estimate=pl.CostEstimate(
            flops=10 * work * HEAD_DIM, bytes_accessed=40 * total * width, transcendentals=work
        ),
        name="attention_back",
    )(g, q, sq, sk, ctx, d_ctx, *kvs)


DEALS = {
    4: (0, 2, 1, 1, 2, 0, 3, 0, 2, 3, 1, 0, 1, 2, 3, 0, 3),
    8: (7, 0, 4, 0, 2, 5, 6, 5, 1, 4, 2, 1, 3, 7, 6, 0, 3),
}


def dealing(G):
    deal = DEALS.get(G) or tuple(h % G for h in range(HEADS))
    return deal, [deal[:h].count(deal[h]) for h in range(HEADS)]


def round_up(n, m):
    return -(-n // m) * m


@functools.lru_cache(maxsize=None)
def tables(G, R):
    deal, slot = dealing(G)
    slots = max(slot) + 1
    width = slots * HEAD_DIM
    cols = 3 * D // R
    rows = D // G

    def pick(features, lo, hi, g):
        return [f for f in range(lo, hi) if deal[(f % D) // HEAD_DIM] == g]

    def place(f):
        section, within = divmod(f, D)
        head, col = divmod(within, HEAD_DIM)
        return section * width + slot[head] * HEAD_DIM + col

    qkv = [[pick(3 * D, d * cols, (d + 1) * cols, g) for g in range(G)] for d in range(R)]
    out = [[pick(D, s * rows, (s + 1) * rows, g) for g in range(G)] for s in range(G)]
    cq = round_up(max(len(p) for line in qkv for p in line), 16)
    co = round_up(max(len(p) for line in out for p in line), 16)
    send_qkv = np.full((R, G, cq), -1, np.int32)
    raw_place = np.full((G, R, cq), -1, np.int32)
    for d in range(R):
        for g in range(G):
            for i, f in enumerate(qkv[d][g]):
                send_qkv[d, g, i] = f - d * cols
                raw_place[g, d, i] = place(f)
    send_out = np.full((G, G, co), -1, np.int32)
    out_place = np.full((G, G, co), -1, np.int32)
    for s in range(G):
        for g in range(G):
            for i, f in enumerate(out[s][g]):
                send_out[s, g, i] = f - s * rows
                out_place[g, s, i] = place(f)
    owned = np.full((G, slots), -1, np.int32)
    for h in range(HEADS):
        owned[deal[h], slot[h]] = h
    return (
        slots,
        owned,
        cq,
        co,
        send_qkv.reshape(R, G * cq),
        raw_place,
        send_out.reshape(G, G * co),
        out_place.reshape(G, G * co),
    )


def one_hot_rows(size, table):
    return (lax.broadcasted_iota(jnp.int32, (size, table.shape[0]), 0) == table[None, :]).astype(BF)


def rotate(x, axis, step):
    count = lax.axis_size(axis)
    return lax.ppermute(x, axis, [(s, (s + step) % count) for s in range(count)])


def gather_rot(x):
    return [x] + [rotate(x, "group", k) for k in range(1, lax.axis_size("group"))]


def scatter_rot(x):
    count = lax.axis_size("group")
    rows = x.shape[0] // count
    total = x[:rows]
    for k in range(1, count):
        piece = x[k * rows : (k + 1) * rows].astype(BF)
        total = total + rotate(piece, "group", -k).astype(F32)
    return total


def gather_group(x):
    return jnp.concatenate(gather_rot(x), axis=0)


def grid_of(R):
    inner = 1
    while 4 * inner * inner <= R:
        inner *= 2
    return R // inner, inner


def shift_dp(x, outer_step, inner_step):
    outer, inner = grid_of(lax.axis_size("dp"))
    return lax.ppermute(
        x,
        "dp",
        [
            (
                o * inner + i,
                (o + outer_step) % outer * inner + (i + inner_step) % inner,
            )
            for o in range(outer)
            for i in range(inner)
        ],
    )


def steps_dp(R):
    outer, inner = grid_of(R)
    return [(a, b) for a in range(outer) for b in range(inner)]


def back_of(d, step, R):
    outer, inner = grid_of(R)
    o = lax.rem(lax.div(d, inner) - step[0] + outer, outer)
    i = lax.rem(lax.rem(d, inner) - step[1] + inner, inner)
    return o * inner + i


def gather_dp(x):
    outer, inner = grid_of(lax.axis_size("dp"))
    blocks = []
    for a in range(outer):
        own = shift_dp(x, a, 0) if a else x
        blocks.append(own)
        for b in range(1, inner):
            blocks.append(shift_dp(own, 0, b))
    return blocks


def scatter_dp(block):
    outer, inner = grid_of(lax.axis_size("dp"))
    total = None
    for a in range(outer - 1, -1, -1):
        part = block((a, 0)).astype(F32)
        for b in range(1, inner):
            part = part + shift_dp(block((a, b)), 0, -b).astype(F32)
        if a:
            part = shift_dp(part.astype(BF), -a, 0).astype(F32)
        total = part if total is None else total + part
    return total


def swap_group(x):
    return lax.all_to_all(x, "group", 0, 0, tiled=True)


def shards(
    tokens,
    cotangent,
    segment_ids,
    w_qkv,
    w_out,
    w_up,
    w_down,
    vectors,
    m_qkv,
    m_out,
    m_up,
    m_down,
    m_vec,
    v_qkv,
    v_out,
    v_up,
    v_down,
    v_vec,
):
    G = lax.axis_size("group")
    R = lax.axis_size("dp")
    g = lax.axis_index("group")
    d = lax.axis_index("dp")
    T = tokens.shape[0]
    B = G * T
    DG = D // G
    DC = D // R
    FC = FF // R
    FS = FC // G
    FG = FF // G
    RG = R // G
    prev = REACH // G
    slots, t_owned, cq, co, t_send_qkv, t_raw, t_send_out, t_out = tables(G, R)
    W = slots * HEAD_DIM
    score_scale = HEAD_DIM ** (-0.5)

    steps = steps_dp(R)

    pick_qkv = one_hot_rows(w_qkv.shape[1], jnp.asarray(t_send_qkv)[d])
    raw_table = jnp.asarray(t_raw)[g].reshape(R * cq)
    pick_q = one_hot_rows(W, raw_table)
    pick_kv = one_hot_rows(2 * W, raw_table - W)
    pick_out = one_hot_rows(DG, jnp.asarray(t_send_out)[g])
    out_pick = one_hot_rows(W, jnp.asarray(t_out)[g])
    fold = DG // DC

    def folded(x):
        return jnp.concatenate(jnp.split(x, fold, axis=1), axis=2)

    def unfolded(x):
        return jnp.concatenate(jnp.split(x, fold, axis=2), axis=1)

    send_qkv = dot(pick_qkv, w_qkv.astype(BF), 0, 1, BF).reshape(G, cq, DG)
    send_vec = jnp.broadcast_to(vectors.astype(BF)[None], (G, 12, DG))
    send_out = folded(dot(pick_out, w_out.astype(BF), 0, 0, BF).reshape(G, co, DC))
    first = swap_group(jnp.concatenate([send_qkv, send_vec, send_out], axis=1))
    mine_qkv = jnp.swapaxes(first[:, :cq], 0, 1).reshape(cq, D)
    vec_full = jnp.swapaxes(first[:, cq : cq + 12], 0, 1).reshape(12, D).astype(F32)
    mine_out = dot(unfolded(first[:, cq + 12 :]).reshape(G * co, DC), out_pick, 0, 1, BF)
    raw_qkv = lax.all_gather(mine_qkv, "dp", axis=0, tiled=True)
    full_out = lax.all_gather(mine_out, "dp", axis=0, tiled=True)

    send_up = w_up.astype(BF).T.reshape(G, FS, DG)
    send_down = jnp.transpose(
        w_down.astype(BF).reshape(RG, G, FS, DC), (1, 3, 0, 2)
    ).reshape(G, FS, DG)
    mine_qkv, second = lax.optimization_barrier(
        (mine_qkv, jnp.concatenate([send_up, send_down], axis=1))
    )
    second = swap_group(second)
    mine_up = jnp.swapaxes(second[:, :FS], 0, 1).reshape(FS, D)
    mine_down = second[:, FS:].reshape(G, DC, RG * FS)
    mine_down = jnp.swapaxes(mine_down, 0, 1).reshape(FS, D)
    norm_gain = vec_full[0]
    norm_shift = vec_full[1]
    bias_query = vec_full[2]
    bias_value = vec_full[3]
    bias_out = vec_full[4]
    gain_two = vec_full[5]
    shift_two = vec_full[6]
    bias_down = vec_full[7]
    bias_up = lax.dynamic_index_in_dim(
        vec_full[8:12].reshape(R, G, FS), g, 1, keepdims=False
    ).reshape(FG)

    seg_plus = segment_ids + 1
    seg_turned = gather_rot(seg_plus)
    seg_own = jnp.zeros((B,), jnp.int32)
    for k, piece in enumerate(seg_turned):
        seg_own = lax.dynamic_update_slice_in_dim(seg_own, piece, lax.rem(g - k + G, G) * T, 0)
    seg_keys = jnp.concatenate(
        [
            lax.ppermute(seg_own, "dp", [(s, s + k) for s in range(R - k)])
            for k in range(prev, 0, -1)
        ]
        + [seg_own]
    )
    window = (REACH + 1) * T
    seg_windows = jnp.stack([seg_keys[i * T : i * T + window] for i in range(G)])[:, None, :]
    seg_queries = jnp.concatenate(seg_turned)[:, None]
    g_here = g.astype(jnp.int32)[None]

    tokens_wide = tokens.astype(F32)
    normed, inv_std = layer_norm(tokens_wide)
    hidden = (normed * norm_gain + norm_shift).astype(BF)
    hidden_all = gather_group(hidden)
    cot_all = gather_group(cotangent)

    raw_qkv, full_out, hidden_all, mine_ff = lax.optimization_barrier(
        (raw_qkv, full_out, hidden_all, jnp.concatenate([mine_up, mine_down], axis=0))
    )
    full_ff = lax.all_gather(mine_ff, "dp", axis=0)
    full_up = full_ff[:, :FS].reshape(R * FS, D)
    full_down = full_ff[:, FS:].reshape(D, FG)

    head_ids = jnp.asarray(t_owned)[g]
    head_pick = (head_ids[:, None] == jnp.arange(HEADS, dtype=jnp.int32)[None, :]).astype(F32)

    def heads_of(vector):
        return jnp.sum(
            head_pick[:, :, None] * vector.reshape(HEADS, HEAD_DIM)[None], axis=1
        ).reshape(W)

    bias_heads = jnp.concatenate(
        [heads_of(bias_query), jnp.zeros((W,), F32), heads_of(bias_value)]
    )[None, :]
    bias_raw = dot(bias_heads[:, :W].astype(BF), pick_q, 1, 0) + dot(
        bias_heads[:, W:].astype(BF), pick_kv, 1, 0
    )
    scale_raw = jnp.where((raw_table >= 0) & (raw_table < W), F32(score_scale), F32(1.0))[None, :]
    qkv_raw = ((dot(hidden_all, raw_qkv, 1, 1) + bias_raw) * scale_raw).astype(BF)
    kv_own = dot(qkv_raw, pick_kv, 1, 1, BF)
    query = dot(qkv_raw, pick_q, 1, 1, BF)
    kvs = [
        lax.ppermute(kv_own, "dp", [(s, s + k) for s in range(R - k)]) for k in range(prev, 0, -1)
    ] + [kv_own]
    context = attention(g_here, query, kvs, seg_queries, seg_windows, T, slots)
    context_b = context.astype(BF)
    attended = scatter_rot(dot(context_b, full_out, 1, 1))
    mid = tokens_wide + (attended + bias_out)
    normed_two, inv_two = layer_norm(mid)
    hidden_two = gather_group((normed_two * gain_two + shift_two).astype(BF))
    pre_act = dot(hidden_two, full_up, 1, 1) + bias_up
    activated, derivative = gelu_parts(pre_act)
    act_b = activated.astype(BF)

    d_act = dot(cot_all, full_down, 1, 0)
    d_pre = d_act * derivative
    d_pre_b = d_pre.astype(BF)
    d_hidden_two = scatter_rot(dot(d_pre_b, full_up, 1, 0))
    cot_wide = cotangent.astype(F32)
    d_mid = cot_wide + norm_back(d_hidden_two * gain_two, normed_two, inv_two)
    d_mid_all = gather_group(d_mid.astype(BF))
    d_context = dot(d_mid_all, full_out, 1, 0)

    down_sum = scatter_rot(dot(act_b, full_down, 1, 1))
    output = (mid + (down_sum + bias_down)).astype(BF)

    part_up = dot(d_pre_b, hidden_two, 0, 0, BF).reshape(R, FS, D)
    part_down = dot(cot_all, act_b, 0, 0, BF).reshape(R, FS, D)
    part_ff = jnp.concatenate([part_up, part_down], axis=1)
    sum_ff = lax.psum_scatter(part_ff, "dp", scatter_dimension=0, tiled=True)[0]

    part_out = dot(d_mid_all, context_b, 0, 0, BF).reshape(R, DC, W)
    d_query, *d_kvs = attention_back(
        g_here, query, kvs, seg_queries, seg_windows, context, d_context, T, slots
    )
    d_query, part_out = lax.optimization_barrier((d_query, part_out))
    d_kv_own = d_kvs[prev]
    for k in range(prev, 0, -1):
        d_kv_own = d_kv_own + lax.ppermute(
            d_kvs[prev - k], "dp", [(s, s - k) for s in range(k, R)]
        ).astype(F32)
    d_qkv = jnp.concatenate([d_query, d_kv_own], axis=1).astype(BF)
    d_raw = dot(d_qkv, jnp.concatenate([pick_q, pick_kv], axis=0), 1, 0, BF)
    part_qkv = dot(d_raw, hidden_all, 0, 0, BF).reshape(R, cq, D)

    sum_qkv = scatter_dp(
        lambda step: lax.dynamic_index_in_dim(part_qkv, back_of(d, step, R), 0, keepdims=False)
    ).astype(BF)
    sum_out = scatter_dp(
        lambda step: lax.dynamic_index_in_dim(part_out, back_of(d, step, R), 0, keepdims=False)
    ).astype(BF)
    d_hidden = scatter_rot(dot(d_raw, raw_qkv, 1, 0))
    input_grad = d_mid + norm_back(d_hidden * norm_gain, normed, inv_std)

    def heads_back(vector):
        return jnp.sum(
            head_pick[:, :, None] * vector.reshape(slots, 1, HEAD_DIM), axis=0
        ).reshape(D)

    own_col = (jnp.arange(G, dtype=jnp.int32) == g)[None, :, None]
    up_vec = jnp.where(own_col, jnp.sum(d_pre, axis=0).reshape(R, 1, FS), F32(0.0)).reshape(4, D)
    vec_total = jnp.concatenate(
        [
            jnp.stack(
                [
                    jnp.sum(d_hidden * normed, axis=0),
                    jnp.sum(d_hidden, axis=0),
                    heads_back(jnp.sum(d_query, axis=0)),
                    heads_back(jnp.sum(d_kv_own[:, W:], axis=0)),
                    jnp.sum(d_mid, axis=0),
                    jnp.sum(d_hidden_two * normed_two, axis=0),
                    jnp.sum(d_hidden_two, axis=0),
                    jnp.sum(cot_wide, axis=0),
                ],
                axis=0,
            ),
            up_vec,
        ],
        axis=0,
    )
    for axis, count in (("group", G), ("dp", R)):
        step = 1
        while step < count:
            vec_total = vec_total + lax.ppermute(
                vec_total, axis, [(s, s ^ step) for s in range(count)]
            )
            step *= 2
    grad_vec = lax.dynamic_slice_in_dim(vec_total, g * DG, DG, 1)

    back_out = dot(out_pick, sum_out, 0, 1, BF).reshape(G, co, DC)
    back_out = folded(back_out)
    back_up = jnp.swapaxes(sum_ff[:FS].reshape(FS, G, DG), 0, 1)
    back_down = jnp.swapaxes(sum_ff[FS:].reshape(DC, G, RG * FS), 0, 1).reshape(G, FS, DG)
    back = swap_group(jnp.concatenate([back_up, back_down], axis=1))
    grad_up = dot(back[:, :FS].reshape(FC, DG), jnp.eye(FC, dtype=BF), 0, 0)
    grad_down = (
        jnp.transpose(back[:, FS:].reshape(G, DC, RG, FS), (2, 0, 3, 1)).reshape(FG, DC).astype(F32)
    )
    new_up, new_m_up, new_v_up = adamw_update(w_up, m_up, v_up, grad_up, 0.1)
    new_down, new_m_down, new_v_down = adamw_update(w_down, m_down, v_down, grad_down, 0.1)
    sum_qkv, grad_up, grad_down, new_up, new_down = lax.optimization_barrier(
        (sum_qkv, grad_up, grad_down, new_up, new_down)
    )
    back_qkv = jnp.swapaxes(sum_qkv.reshape(cq, G, DG), 0, 1)
    last = swap_group(jnp.concatenate([back_qkv, back_out], axis=1))
    grad_qkv = dot(last[:, :cq].reshape(G * cq, DG), pick_qkv, 0, 1)
    grad_out = dot(pick_out, unfolded(last[:, cq:]).reshape(G * co, DC), 1, 0)

    new_qkv, new_m_qkv, new_v_qkv = adamw_update(w_qkv, m_qkv, v_qkv, grad_qkv, 0.1)
    new_out, new_m_out, new_v_out = adamw_update(w_out, m_out, v_out, grad_out, 0.1)
    new_vec, new_m_vec, new_v_vec = adamw_update(vectors, m_vec, v_vec, grad_vec, 0.0)
    return (
        output,
        input_grad,
        grad_qkv,
        grad_out,
        grad_up,
        grad_down,
        grad_vec,
        new_qkv,
        new_out,
        new_up,
        new_down,
        new_vec,
        new_m_qkv,
        new_m_out,
        new_m_up,
        new_m_down,
        new_m_vec,
        new_v_qkv,
        new_v_out,
        new_v_up,
        new_v_down,
        new_v_vec,
    )


def solution(mesh):
    rows, mat, vec = P(("dp", "group"), None), P("group", "dp"), P(None, "group")
    state = (mat, mat, mat, mat, vec)
    in_specs = (rows, rows, P(("dp", "group"))) + state * 3
    out_specs = (rows, rows) + state * 4
    return jax.shard_map(shards, mesh=mesh, in_specs=in_specs, out_specs=out_specs, check_vma=False)
```

```python
import functools

import jax
import jax.numpy as jnp
import numpy as np
from jax import lax
from jax.experimental import pallas as pl
from jax.experimental.pallas import tpu as pltpu
from jax.sharding import PartitionSpec as P

D = 1088
HEADS = 17
HEAD_DIM = 64
FF = 4352
ADAM_STEP = 3
REACH = 8
BF = jnp.bfloat16
F32 = jnp.float32


def layer_norm(rows):
    mean_rows = jnp.mean(rows, axis=-1, keepdims=True)
    centered = rows - mean_rows
    variance = jnp.mean(centered * centered, axis=-1, keepdims=True)
    inv_std = lax.rsqrt(variance + 1e-05)
    return (centered * inv_std, inv_std)


def norm_back(d_normed, normed, inv_std):
    return inv_std * (
        d_normed
        - jnp.mean(d_normed, axis=-1, keepdims=True)
        - normed * jnp.mean(d_normed * normed, axis=-1, keepdims=True)
    )


def gelu_parts(pre_act):
    gelu_scale = 0.7978845608028654
    cubic_term = 0.044715 * pre_act * pre_act
    argument = gelu_scale * pre_act * (1.0 + cubic_term)
    tangent = jnp.tanh(argument)
    activated = 0.5 * pre_act * (1.0 + tangent)
    derivative = 0.5 * (1.0 + tangent) + 0.5 * pre_act * (1.0 - tangent * tangent) * gelu_scale * (
        1.0 + 3.0 * cubic_term
    )
    return (activated, derivative)


def adamw_update(weight_now, first_mom, second_mom, gradient, decay_rate):
    new_first = 0.9 * first_mom + 0.1 * gradient
    new_second = 0.999 * second_mom + 0.001 * gradient * gradient
    step_size = (
        new_first
        / (1.0 - 0.9**ADAM_STEP)
        / (jnp.sqrt(new_second / (1.0 - 0.999**ADAM_STEP)) + 1e-08)
    )
    return (weight_now - 0.03 * (step_size + decay_rate * weight_now), new_first, new_second)


def dot(a, b, ca, cb, out=F32):
    return lax.dot_general(a, b, (((ca,), (cb,)), ((), ())), preferred_element_type=out)


def scores_of(q, k, same, first):
    s = lax.dot_general(q, k, (((1,), (1,)), ((), ())), preferred_element_type=F32)
    rows = lax.broadcasted_iota(jnp.int32, s.shape, 0)
    cols = lax.broadcasted_iota(jnp.int32, s.shape, 1)
    return jnp.where(same & (cols <= rows + first), jnp.exp(s), F32(0.0))


def in_order_rows(g, G, T, refs, scratch):
    for n, ref in enumerate(refs):
        for j in range(G):
            at = pl.multiple_of(lax.rem(g - j + G, G) * T, T)
            scratch[(n * G + j) * T : (n * G + j + 1) * T, :] = ref[pl.ds(at, T), :]


def attn_fwd_kernel(heads, G, g_ref, q_ref, sq_ref, sk_ref, *refs):
    kv_refs, ctx_ref, kvs = refs[:-2], refs[-2], refs[-1]
    rows = q_ref.shape[0]
    width = heads * HEAD_DIM
    window = sk_ref.shape[2]

    @pl.when(pl.program_id(0) == 0)
    def _():
        in_order_rows(g_ref[0], G, rows, kv_refs, kvs)

    at = pl.ds(pl.multiple_of(pl.program_id(0) * rows, rows), window)
    same = sq_ref[...] == sk_ref[0]
    for h in range(heads):
        lanes = slice(h * HEAD_DIM, (h + 1) * HEAD_DIM)
        lanes_v = slice(width + h * HEAD_DIM, width + (h + 1) * HEAD_DIM)
        w = scores_of(q_ref[:, lanes], kvs[at, lanes], same, window - rows)
        den = jnp.sum(w, axis=1, keepdims=True)
        num = jnp.dot(w.astype(BF), kvs[at, lanes_v], preferred_element_type=F32)
        ctx_ref[:, lanes] = num / den


def attn_bwd_kernel(heads, G, parts, g_ref, q_ref, sq_ref, sk_ref, ctx_ref, dc_ref, *refs):
    kv_refs = refs[:parts]
    dq_ref = refs[parts]
    dkv_refs = refs[parts + 1 : 2 * parts + 1]
    kvs, dkvs = refs[2 * parts + 1 :]
    rows = q_ref.shape[0]
    width = heads * HEAD_DIM
    window = sk_ref.shape[2]
    g = g_ref[0]

    @pl.when(pl.program_id(0) == 0)
    def _():
        in_order_rows(g, G, rows, kv_refs, kvs)
        dkvs[...] = jnp.zeros_like(dkvs)

    at = pl.ds(pl.multiple_of(pl.program_id(0) * rows, rows), window)
    same = sq_ref[...] == sk_ref[0]
    for h in range(heads):
        lanes = slice(h * HEAD_DIM, (h + 1) * HEAD_DIM)
        lanes_v = slice(width + h * HEAD_DIM, width + (h + 1) * HEAD_DIM)
        q = q_ref[:, lanes]
        k = kvs[at, lanes]
        dc = dc_ref[:, lanes]
        w = scores_of(q, k, same, window - rows)
        p = w * (1.0 / jnp.sum(w, axis=1, keepdims=True))
        delta = jnp.sum(dc * ctx_ref[:, lanes], axis=1, keepdims=True)
        dc_b = dc.astype(BF)
        dp = dot(dc_b, kvs[at, lanes_v], 1, 1)
        ds = (p * (dp - delta)).astype(BF)
        dq_ref[:, lanes] = jnp.dot(ds, k, preferred_element_type=F32) * (HEAD_DIM**-0.5)
        dkvs[at, lanes] += dot(ds, q, 0, 0)
        dkvs[at, lanes_v] += dot(p.astype(BF), dc_b, 0, 0)

    @pl.when(pl.program_id(0) == G - 1)
    def _():
        for n, ref in enumerate(dkv_refs):
            for j in range(G):
                to = pl.multiple_of(lax.rem(g - j + G, G) * rows, rows)
                part = dkvs[(n * G + j) * rows : (n * G + j + 1) * rows, :]
                ref[pl.ds(to, rows), :] = part.astype(ref.dtype)


def attn_specs(G, T, width, window):
    turned = lambda i, g: (lax.rem(g[0] - i + G, G), 0)
    row = pl.BlockSpec((T, width), turned)
    full = pl.BlockSpec((G * T, 2 * width), lambda i, g: (0, 0))
    sq = pl.BlockSpec((T, 1), turned)
    sk = pl.BlockSpec((1, 1, window), lambda i, g: (i, 0, 0))
    return row, full, sq, sk


def attention(g, q, kvs, sq, sk, T, heads):
    total, width = q.shape
    G, window = total // T, sk.shape[2]
    row, full, sqs, sks = attn_specs(G, T, width, window)
    work = total * window * heads
    return pl.pallas_call(
        functools.partial(attn_fwd_kernel, heads, G),
        grid_spec=pltpu.PrefetchScalarGridSpec(
            num_scalar_prefetch=1,
            grid=(G,),
            in_specs=[row, sqs, sks] + [full] * len(kvs),
            out_specs=row,
            scratch_shapes=[pltpu.VMEM((len(kvs) * total, 2 * width), BF)],
        ),
        out_shape=jax.ShapeDtypeStruct((total, width), F32),
        cost_estimate=pl.CostEstimate(
            flops=4 * work * HEAD_DIM, bytes_accessed=18 * total * width, transcendentals=work
        ),
        name="attention",
    )(g, q, sq, sk, *kvs)


def attention_back(g, q, kvs, sq, sk, ctx, d_ctx, T, heads):
    total, width = q.shape
    G, window = total // T, sk.shape[2]
    parts = len(kvs)
    row, full, sqs, sks = attn_specs(G, T, width, window)
    work = total * window * heads
    return pl.pallas_call(
        functools.partial(attn_bwd_kernel, heads, G, parts),
        grid_spec=pltpu.PrefetchScalarGridSpec(
            num_scalar_prefetch=1,
            grid=(G,),
            in_specs=[row, sqs, sks, row, row] + [full] * parts,
            out_specs=[row] + [full] * parts,
            scratch_shapes=[
                pltpu.VMEM((parts * total, 2 * width), BF),
                pltpu.VMEM((parts * total, 2 * width), F32),
            ],
        ),
        out_shape=[jax.ShapeDtypeStruct((total, width), F32)]
        + [
            jax.ShapeDtypeStruct((total, 2 * width), F32 if n == parts - 1 else BF)
            for n in range(parts)
        ],
        cost_estimate=pl.CostEstimate(
            flops=10 * work * HEAD_DIM, bytes_accessed=40 * total * width, transcendentals=work
        ),
        name="attention_back",
    )(g, q, sq, sk, ctx, d_ctx, *kvs)


DEALS = {
    4: (0, 2, 1, 1, 2, 0, 3, 0, 2, 3, 1, 0, 1, 2, 3, 0, 3),
    8: (7, 0, 4, 0, 2, 5, 6, 5, 1, 4, 2, 1, 3, 7, 6, 0, 3),
}


def dealing(G):
    deal = DEALS.get(G) or tuple(h % G for h in range(HEADS))
    return deal, [deal[:h].count(deal[h]) for h in range(HEADS)]


def round_up(n, m):
    return -(-n // m) * m


@functools.lru_cache(maxsize=None)
def tables(G, R):
    deal, slot = dealing(G)
    slots = max(slot) + 1
    width = slots * HEAD_DIM
    cols = 3 * D // R
    rows = D // G

    def pick(features, lo, hi, g):
        return [f for f in range(lo, hi) if deal[(f % D) // HEAD_DIM] == g]

    def place(f):
        section, within = divmod(f, D)
        head, col = divmod(within, HEAD_DIM)
        return section * width + slot[head] * HEAD_DIM + col

    qkv = [[pick(3 * D, d * cols, (d + 1) * cols, g) for g in range(G)] for d in range(R)]
    out = [[pick(D, s * rows, (s + 1) * rows, g) for g in range(G)] for s in range(G)]
    cq = round_up(max(len(p) for line in qkv for p in line), 16)
    co = round_up(max(len(p) for line in out for p in line), 16)
    send_qkv = np.full((R, G, cq), -1, np.int32)
    raw_place = np.full((G, R, cq), -1, np.int32)
    for d in range(R):
        for g in range(G):
            for i, f in enumerate(qkv[d][g]):
                send_qkv[d, g, i] = f - d * cols
                raw_place[g, d, i] = place(f)
    send_out = np.full((G, G, co), -1, np.int32)
    out_place = np.full((G, G, co), -1, np.int32)
    for s in range(G):
        for g in range(G):
            for i, f in enumerate(out[s][g]):
                send_out[s, g, i] = f - s * rows
                out_place[g, s, i] = place(f)
    owned = np.full((G, slots), -1, np.int32)
    for h in range(HEADS):
        owned[deal[h], slot[h]] = h
    return (
        slots,
        owned,
        cq,
        co,
        send_qkv.reshape(R, G * cq),
        raw_place,
        send_out.reshape(G, G * co),
        out_place.reshape(G, G * co),
    )


def one_hot_rows(size, table):
    return (lax.broadcasted_iota(jnp.int32, (size, table.shape[0]), 0) == table[None, :]).astype(BF)


def rotate(x, axis, step):
    count = lax.axis_size(axis)
    return lax.ppermute(x, axis, [(s, (s + step) % count) for s in range(count)])


def gather_rot(x):
    return [x] + [rotate(x, "group", k) for k in range(1, lax.axis_size("group"))]


def scatter_rot(x):
    count = lax.axis_size("group")
    rows = x.shape[0] // count
    total = x[:rows]
    for k in range(1, count):
        piece = x[k * rows : (k + 1) * rows].astype(BF)
        total = total + rotate(piece, "group", -k).astype(F32)
    return total


def gather_group(x):
    return jnp.concatenate(gather_rot(x), axis=0)


def grid_of(R):
    inner = 1
    while 4 * inner * inner <= R:
        inner *= 2
    return R // inner, inner


def shift_dp(x, outer_step, inner_step):
    outer, inner = grid_of(lax.axis_size("dp"))
    return lax.ppermute(
        x,
        "dp",
        [
            (
                o * inner + i,
                (o + outer_step) % outer * inner + (i + inner_step) % inner,
            )
            for o in range(outer)
            for i in range(inner)
        ],
    )


def steps_dp(R):
    outer, inner = grid_of(R)
    return [(a, b) for a in range(outer) for b in range(inner)]


def back_of(d, step, R):
    outer, inner = grid_of(R)
    o = lax.rem(lax.div(d, inner) - step[0] + outer, outer)
    i = lax.rem(lax.rem(d, inner) - step[1] + inner, inner)
    return o * inner + i


def gather_dp(x):
    outer, inner = grid_of(lax.axis_size("dp"))
    blocks = []
    for a in range(outer):
        own = shift_dp(x, a, 0) if a else x
        blocks.append(own)
        for b in range(1, inner):
            blocks.append(shift_dp(own, 0, b))
    return blocks


def scatter_dp(block):
    outer, inner = grid_of(lax.axis_size("dp"))
    total = None
    for a in range(outer - 1, -1, -1):
        part = block((a, 0)).astype(F32)
        for b in range(1, inner):
            part = part + shift_dp(block((a, b)), 0, -b).astype(F32)
        if a:
            part = shift_dp(part.astype(BF), -a, 0).astype(F32)
        total = part if total is None else total + part
    return total


def swap_group(x):
    return lax.all_to_all(x, "group", 0, 0, tiled=True)


def shards(
    tokens,
    cotangent,
    segment_ids,
    w_qkv,
    w_out,
    w_up,
    w_down,
    vectors,
    m_qkv,
    m_out,
    m_up,
    m_down,
    m_vec,
    v_qkv,
    v_out,
    v_up,
    v_down,
    v_vec,
):
    G = lax.axis_size("group")
    R = lax.axis_size("dp")
    g = lax.axis_index("group")
    d = lax.axis_index("dp")
    T = tokens.shape[0]
    B = G * T
    DG = D // G
    DC = D // R
    FC = FF // R
    FS = FC // G
    FG = FF // G
    RG = R // G
    prev = REACH // G
    slots, t_owned, cq, co, t_send_qkv, t_raw, t_send_out, t_out = tables(G, R)
    W = slots * HEAD_DIM
    score_scale = HEAD_DIM ** (-0.5)

    steps = steps_dp(R)

    pick_qkv = one_hot_rows(w_qkv.shape[1], jnp.asarray(t_send_qkv)[d])
    raw_table = jnp.asarray(t_raw)[g].reshape(R * cq)
    pick_q = one_hot_rows(W, raw_table)
    pick_kv = one_hot_rows(2 * W, raw_table - W)
    pick_out = one_hot_rows(DG, jnp.asarray(t_send_out)[g])
    out_pick = one_hot_rows(W, jnp.asarray(t_out)[g])
    fold = DG // DC

    def folded(x):
        return jnp.concatenate(jnp.split(x, fold, axis=1), axis=2)

    def unfolded(x):
        return jnp.concatenate(jnp.split(x, fold, axis=2), axis=1)

    send_qkv = dot(pick_qkv, w_qkv.astype(BF), 0, 1, BF).reshape(G, cq, DG)
    send_vec = jnp.broadcast_to(vectors.astype(BF)[None], (G, 12, DG))
    send_out = folded(dot(pick_out, w_out.astype(BF), 0, 0, BF).reshape(G, co, DC))
    first = swap_group(jnp.concatenate([send_qkv, send_vec, send_out], axis=1))
    mine_qkv = jnp.swapaxes(first[:, :cq], 0, 1).reshape(cq, D)
    vec_full = jnp.swapaxes(first[:, cq : cq + 12], 0, 1).reshape(12, D).astype(F32)
    mine_out = dot(unfolded(first[:, cq + 12 :]).reshape(G * co, DC), out_pick, 0, 1, BF)
    raw_qkv = lax.all_gather(mine_qkv, "dp", axis=0, tiled=True)
    full_out = lax.all_gather(mine_out, "dp", axis=0, tiled=True)

    send_up = w_up.astype(BF).T.reshape(G, FS, DG)
    send_down = jnp.transpose(
        w_down.astype(BF).reshape(RG, G, FS, DC), (1, 3, 0, 2)
    ).reshape(G, FS, DG)
    mine_qkv, second = lax.optimization_barrier(
        (mine_qkv, jnp.concatenate([send_up, send_down], axis=1))
    )
    second = swap_group(second)
    mine_up = jnp.swapaxes(second[:, :FS], 0, 1).reshape(FS, D)
    mine_down = second[:, FS:].reshape(G, DC, RG * FS)
    mine_down = jnp.swapaxes(mine_down, 0, 1).reshape(FS, D)
    norm_gain = vec_full[0]
    norm_shift = vec_full[1]
    bias_query = vec_full[2]
    bias_value = vec_full[3]
    bias_out = vec_full[4]
    gain_two = vec_full[5]
    shift_two = vec_full[6]
    bias_down = vec_full[7]
    bias_up = lax.dynamic_index_in_dim(
        vec_full[8:12].reshape(R, G, FS), g, 1, keepdims=False
    ).reshape(FG)

    seg_plus = segment_ids + 1
    seg_turned = gather_rot(seg_plus)
    seg_own = jnp.zeros((B,), jnp.int32)
    for k, piece in enumerate(seg_turned):
        seg_own = lax.dynamic_update_slice_in_dim(seg_own, piece, lax.rem(g - k + G, G) * T, 0)
    seg_keys = jnp.concatenate(
        [
            lax.ppermute(seg_own, "dp", [(s, s + k) for s in range(R - k)])
            for k in range(prev, 0, -1)
        ]
        + [seg_own]
    )
    window = (REACH + 1) * T
    seg_queries = jnp.concatenate(seg_turned)[:, None]
    g_here = g.astype(jnp.int32)[None]

    tokens_wide = tokens.astype(F32)
    normed, inv_std = layer_norm(tokens_wide)
    hidden = (normed * norm_gain + norm_shift).astype(BF)
    hidden_all = gather_group(hidden)
    cot_all = gather_group(cotangent)

    raw_qkv, full_out, hidden_all, seg_keys, mine_ff = lax.optimization_barrier(
        (raw_qkv, full_out, hidden_all, seg_keys, jnp.concatenate([mine_up, mine_down], axis=0))
    )
    seg_windows = jnp.stack([seg_keys[i * T : i * T + window] for i in range(G)])[:, None, :]
    full_ff = lax.all_gather(mine_ff, "dp", axis=0)
    full_up = full_ff[:, :FS].reshape(R * FS, D)
    full_down = full_ff[:, FS:].reshape(D, FG)

    head_ids = jnp.asarray(t_owned)[g]
    head_pick = (head_ids[:, None] == jnp.arange(HEADS, dtype=jnp.int32)[None, :]).astype(F32)

    def heads_of(vector):
        return jnp.sum(
            head_pick[:, :, None] * vector.reshape(HEADS, HEAD_DIM)[None], axis=1
        ).reshape(W)

    bias_heads = jnp.concatenate(
        [heads_of(bias_query), jnp.zeros((W,), F32), heads_of(bias_value)]
    )[None, :]
    bias_raw = dot(bias_heads[:, :W].astype(BF), pick_q, 1, 0) + dot(
        bias_heads[:, W:].astype(BF), pick_kv, 1, 0
    )
    scale_raw = jnp.where((raw_table >= 0) & (raw_table < W), F32(score_scale), F32(1.0))[None, :]
    qkv_raw = ((dot(hidden_all, raw_qkv, 1, 1) + bias_raw) * scale_raw).astype(BF)
    kv_own = dot(qkv_raw, pick_kv, 1, 1, BF)
    query = dot(qkv_raw, pick_q, 1, 1, BF)
    kvs = [
        lax.ppermute(kv_own, "dp", [(s, s + k) for s in range(R - k)]) for k in range(prev, 0, -1)
    ] + [kv_own]
    context = attention(g_here, query, kvs, seg_queries, seg_windows, T, slots)
    context_b = context.astype(BF)
    attended = scatter_rot(dot(context_b, full_out, 1, 1))
    mid = tokens_wide + (attended + bias_out)
    normed_two, inv_two = layer_norm(mid)
    hidden_two = gather_group((normed_two * gain_two + shift_two).astype(BF))
    pre_act = dot(hidden_two, full_up, 1, 1) + bias_up
    activated, derivative = gelu_parts(pre_act)
    act_b = activated.astype(BF)

    d_act = dot(cot_all, full_down, 1, 0)
    d_pre = d_act * derivative
    d_pre_b = d_pre.astype(BF)
    d_hidden_two = scatter_rot(dot(d_pre_b, full_up, 1, 0))
    cot_wide = cotangent.astype(F32)
    d_mid = cot_wide + norm_back(d_hidden_two * gain_two, normed_two, inv_two)
    d_mid_all = gather_group(d_mid.astype(BF))
    d_context = dot(d_mid_all, full_out, 1, 0)

    down_sum = scatter_rot(dot(act_b, full_down, 1, 1))
    output = (mid + (down_sum + bias_down)).astype(BF)

    part_up = dot(d_pre_b, hidden_two, 0, 0, BF).reshape(R, FS, D)
    part_down = dot(cot_all, act_b, 0, 0, BF).reshape(R, FS, D)
    part_ff = jnp.concatenate([part_up, part_down], axis=1)
    sum_ff = lax.psum_scatter(part_ff, "dp", scatter_dimension=0, tiled=True)[0]

    part_out = dot(d_mid_all, context_b, 0, 0, BF).reshape(R, DC, W)
    d_query, *d_kvs = attention_back(
        g_here, query, kvs, seg_queries, seg_windows, context, d_context, T, slots
    )
    d_query, part_out = lax.optimization_barrier((d_query, part_out))
    d_kv_own = d_kvs[prev]
    for k in range(prev, 0, -1):
        d_kv_own = d_kv_own + lax.ppermute(
            d_kvs[prev - k], "dp", [(s, s - k) for s in range(k, R)]
        ).astype(F32)
    d_qkv = jnp.concatenate([d_query, d_kv_own], axis=1).astype(BF)
    d_raw = dot(d_qkv, jnp.concatenate([pick_q, pick_kv], axis=0), 1, 0, BF)
    part_qkv = dot(d_raw, hidden_all, 0, 0, BF).reshape(R, cq, D)

    sum_qkv = scatter_dp(
        lambda step: lax.dynamic_index_in_dim(part_qkv, back_of(d, step, R), 0, keepdims=False)
    ).astype(BF)
    sum_out = scatter_dp(
        lambda step: lax.dynamic_index_in_dim(part_out, back_of(d, step, R), 0, keepdims=False)
    ).astype(BF)
    d_hidden = scatter_rot(dot(d_raw, raw_qkv, 1, 0))
    input_grad = d_mid + norm_back(d_hidden * norm_gain, normed, inv_std)

    def heads_back(vector):
        return jnp.sum(
            head_pick[:, :, None] * vector.reshape(slots, 1, HEAD_DIM), axis=0
        ).reshape(D)

    own_col = (jnp.arange(G, dtype=jnp.int32) == g)[None, :, None]
    up_vec = jnp.where(own_col, jnp.sum(d_pre, axis=0).reshape(R, 1, FS), F32(0.0)).reshape(4, D)
    vec_total = jnp.concatenate(
        [
            jnp.stack(
                [
                    jnp.sum(d_hidden * normed, axis=0),
                    jnp.sum(d_hidden, axis=0),
                    heads_back(jnp.sum(d_query, axis=0)),
                    heads_back(jnp.sum(d_kv_own[:, W:], axis=0)),
                    jnp.sum(d_mid, axis=0),
                    jnp.sum(d_hidden_two * normed_two, axis=0),
                    jnp.sum(d_hidden_two, axis=0),
                    jnp.sum(cot_wide, axis=0),
                ],
                axis=0,
            ),
            up_vec,
        ],
        axis=0,
    )
    for axis, count in (("group", G), ("dp", R)):
        step = 1
        while step < count:
            vec_total = vec_total + lax.ppermute(
                vec_total, axis, [(s, s ^ step) for s in range(count)]
            )
            step *= 2
    grad_vec = lax.dynamic_slice_in_dim(vec_total, g * DG, DG, 1)

    back_out = dot(out_pick, sum_out, 0, 1, BF).reshape(G, co, DC)
    back_out = folded(back_out)
    back_up = jnp.swapaxes(sum_ff[:FS].reshape(FS, G, DG), 0, 1)
    back_down = jnp.swapaxes(sum_ff[FS:].reshape(DC, G, RG * FS), 0, 1).reshape(G, FS, DG)
    back = swap_group(jnp.concatenate([back_up, back_down], axis=1))
    grad_up = dot(back[:, :FS].reshape(FC, DG), jnp.eye(FC, dtype=BF), 0, 0)
    grad_down = (
        jnp.transpose(back[:, FS:].reshape(G, DC, RG, FS), (2, 0, 3, 1)).reshape(FG, DC).astype(F32)
    )
    new_up, new_m_up, new_v_up = adamw_update(w_up, m_up, v_up, grad_up, 0.1)
    new_down, new_m_down, new_v_down = adamw_update(w_down, m_down, v_down, grad_down, 0.1)
    sum_qkv, grad_up, grad_down, new_up, new_down = lax.optimization_barrier(
        (sum_qkv, grad_up, grad_down, new_up, new_down)
    )
    back_qkv = jnp.swapaxes(sum_qkv.reshape(cq, G, DG), 0, 1)
    last = swap_group(jnp.concatenate([back_qkv, back_out], axis=1))
    grad_qkv = dot(last[:, :cq].reshape(G * cq, DG), pick_qkv, 0, 1)
    grad_out = dot(pick_out, unfolded(last[:, cq:]).reshape(G * co, DC), 1, 0)

    new_qkv, new_m_qkv, new_v_qkv = adamw_update(w_qkv, m_qkv, v_qkv, grad_qkv, 0.1)
    new_out, new_m_out, new_v_out = adamw_update(w_out, m_out, v_out, grad_out, 0.1)
    new_vec, new_m_vec, new_v_vec = adamw_update(vectors, m_vec, v_vec, grad_vec, 0.0)
    return (
        output,
        input_grad,
        grad_qkv,
        grad_out,
        grad_up,
        grad_down,
        grad_vec,
        new_qkv,
        new_out,
        new_up,
        new_down,
        new_vec,
        new_m_qkv,
        new_m_out,
        new_m_up,
        new_m_down,
        new_m_vec,
        new_v_qkv,
        new_v_out,
        new_v_up,
        new_v_down,
        new_v_vec,
    )


def solution(mesh):
    rows, mat, vec = P(("dp", "group"), None), P("group", "dp"), P(None, "group")
    state = (mat, mat, mat, mat, vec)
    in_specs = (rows, rows, P(("dp", "group"))) + state * 3
    out_specs = (rows, rows) + state * 4
    return jax.shard_map(shards, mesh=mesh, in_specs=in_specs, out_specs=out_specs, check_vma=False)
```
